128 devices in a mesh: blk: 64 (over x_lo, y, z, core), grp: 2 (over x_hi).
Axes of the slice: x: 4 (x_hi: 2, x_lo: 2; x = x_hi * 2 + x_lo), y: 4, z: 4, core: 2. Of those that a mesh axis runs over, the one named last changes fastest.
Arguments:
- star_state: float32 [13, 32768], P(None, 'blk')
- active_local: int32 [8192], P(('blk', 'grp')), may hold values from 0 to 511, as said below
- neighbours: int32 [8192, 64], P(('blk', 'grp')), may hold values from 0 to 32767, as said below
- counts: int32 [8192], P(('blk', 'grp')), may hold values from 1 to 64, as said below
Outputs:
- new_state: float32 [6, 8192], P(None, ('blk', 'grp'))
- regular: float32 [6, 8192], P(None, ('blk', 'grp'))
- irregular: float32 [6, 8192], P(None, ('blk', 'grp'))
The draws below stay inside these ranges and needn't reach their ends.
Inputs may be any that keep to these rules, and one draw needn't show every extreme that they name: `active_local`: distinct within one blk index over its grp devices. Some device's actives all have counts 64. `neighbours`: over one device's live entries (k < counts), each blk index owns (id // 512) at most 64 of them, reached on some device; entries at k >= counts name the active itself.
All inputs are finite; a program needn't handle non-finite values.
Results may differ from the reference program's by a relative error of at most 0.00002.
Values sent between devices are 32-bit elements; how exact they have to be, the bound alone decides.
No kernel may reach another device: no remote copies, remote signals or barrier semaphores. Data moves between devices by JAX's collectives and lax.ppermute only.
A program may use at most 128 MiB of HBM per device.

```python
import math
import jax
import jax.numpy as jnp
from jax import lax

FIELD_DEV = 512
A_DEV = 64
NB = 64
CLSZ = 16
STARS = 32768
ACTIVES = 8192
N_BLK = 64
N_GRP = 2


def coarse_layout(key):
    layout_key = jax.random.fold_in(key, 303)
    coarse_cell = jax.vmap(lambda subkey: jax.random.permutation(subkey, FIELD_DEV))(jax.random.split(layout_key, N_BLK)).astype(jnp.int32)
    shard_rows = jnp.broadcast_to(jnp.arange(N_BLK, dtype=jnp.int32)[:, None], (N_BLK, FIELD_DEV))
    field_values = jnp.broadcast_to(jnp.arange(FIELD_DEV, dtype=jnp.int32)[None, :], (N_BLK, FIELD_DEV))
    field_at = jnp.zeros((N_BLK, FIELD_DEV), jnp.int32).at[shard_rows, coarse_cell].set(field_values)
    return (coarse_cell, field_at)


def integer_parts(key):
    base_key = jax.random.fold_in(key, 101)
    subkeys = jax.random.split(base_key, 6)
    devices = N_BLK * N_GRP
    coarse_cell, field_at = coarse_layout(key)
    shard_perms = jax.vmap(lambda subkey: jax.random.permutation(subkey, FIELD_DEV))(jax.random.split(subkeys[0], N_BLK))
    active_local = shard_perms[:, :N_GRP * A_DEV].reshape(devices, A_DEV).astype(jnp.int32)
    upper_count = jax.random.randint(subkeys[1], (devices,), NB // 2, NB + 1)
    full_device = jax.random.randint(subkeys[2], (), 0, devices)
    marker = jnp.arange(devices) == full_device
    upper_count = jnp.where(marker, NB, upper_count)
    lower_count = jnp.where(marker, NB, jnp.maximum(1, upper_count // 2))
    random_bits = jax.random.randint(subkeys[3], (devices, A_DEV), 0, 1 << 20)
    counts = lower_count[:, None] + random_bits % (upper_count - lower_count + 1)[:, None]
    live_mask = jnp.arange(NB)[None, None, :] < counts[:, :, None]
    live_order = jnp.cumsum(live_mask.reshape(devices, A_DEV * NB).astype(jnp.int32), axis=1) - 1
    owner_perm = jax.vmap(lambda subkey: jax.random.permutation(subkey, N_BLK))(jax.random.split(subkeys[4], devices))
    owner_blk = jnp.take_along_axis(owner_perm, jnp.maximum(live_order, 0) % N_BLK, axis=1).reshape(devices, A_DEV, NB).astype(jnp.int32)
    home_shard = jnp.arange(devices, dtype=jnp.int32) // N_GRP
    home_blk = home_shard[:, None, None]
    home_cells = jnp.take_along_axis(coarse_cell[home_shard], active_local, axis=1)
    member = jax.random.randint(subkeys[5], (devices, A_DEV, NB), 0, CLSZ)
    target_cell = (home_cells // CLSZ)[:, :, None] * CLSZ + member
    near_field = field_at[owner_blk, target_cell]
    near_ids = owner_blk * FIELD_DEV + near_field
    itself = home_blk * FIELD_DEV + active_local[:, :, None]
    neighbours = jnp.where(live_mask, near_ids, itself)
    return (active_local.reshape(-1).astype(jnp.int32), neighbours.reshape(devices * A_DEV, NB).astype(jnp.int32), counts.reshape(-1).astype(jnp.int32))


def draw_active_local(key, part):
    return integer_parts(key)[0]


def draw_neighbours(key, part):
    return integer_parts(key)[1]


def draw_counts(key, part):
    return integer_parts(key)[2]


def lattice_cells(star_index, total_count):
    bit_total = max(1, (total_count - 1).bit_length())
    lattice = [jnp.zeros_like(star_index), jnp.zeros_like(star_index), jnp.zeros_like(star_index)]
    extents = [1, 1, 1]
    for bit_pos in range(bit_total):
        axis_pick = bit_pos % 3
        depth_level = bit_pos // 3
        lattice[axis_pick] = lattice[axis_pick] + star_index // 2 ** bit_pos % 2 * 2 ** depth_level
        extents[axis_pick] = 2 ** (depth_level + 1)
    return (lattice, extents)


def draw_star_state(key, part):
    subkeys = jax.random.split(jax.random.fold_in(key, 202), 6)
    coarse_cell, field_at = coarse_layout(key)
    star_index = jnp.arange(STARS, dtype=jnp.int32)
    shard_index = star_index // FIELD_DEV
    cell_index = coarse_cell.reshape(-1)
    outer, outer_ext = lattice_cells(cell_index, FIELD_DEV)
    inner, inner_ext = lattice_cells(shard_index, N_BLK)
    spans = [outer_ext[0] * inner_ext[0], outer_ext[1] * inner_ext[1], outer_ext[2] * inner_ext[2]]
    spacing = 2.0 / max(spans)
    jitter = jnp.clip(0.15 * jax.random.normal(subkeys[1], (3, STARS), jnp.float32), -0.4, 0.4)
    velocity = 0.5 * jax.random.normal(subkeys[2], (3, STARS), jnp.float32)
    masses = jnp.exp(jax.random.uniform(subkeys[5], (1, STARS), jnp.float32, math.log(0.25), math.log(4.0))) / STARS
    rows = []
    for axis_pick in range(3):
        cell = outer[axis_pick] * inner_ext[axis_pick] + inner[axis_pick]
        rows.append((cell.astype(jnp.float32) + 0.5 - 0.5 * spans[axis_pick] + jitter[axis_pick]) * spacing)
    position = jnp.stack(rows, axis=0)
    accel_rows = jax.random.normal(subkeys[3], (3, STARS), jnp.float32)
    jerk_rows = jax.random.normal(subkeys[4], (3, STARS), jnp.float32)
    return jnp.concatenate([position, velocity, accel_rows, jerk_rows, masses], axis=0)


def setup_inputs(seed: int = 0) -> dict:
    key_list = jax.random.split(jax.random.key(seed), 5)
    return {
        "star_state": draw_star_state(jax.random.fold_in(key_list[4], 71), 0),
        "active_local": draw_active_local(jax.random.fold_in(key_list[4], 71), 0),
        "neighbours": draw_neighbours(jax.random.fold_in(key_list[4], 71), 0),
        "counts": draw_counts(jax.random.fold_in(key_list[4], 71), 0),
    }


time_step = 0.0078125
soften_sq = 0.001

def pair_terms(pos_self, vel_self, pos_other, vel_other, mass_other):
    offset_pos = pos_other - pos_self
    rel_vel = vel_other - vel_self
    dist_sq = offset_pos[0] * offset_pos[0] + offset_pos[1] * offset_pos[1] + offset_pos[2] * offset_pos[2] + soften_sq
    inverse = 1.0 / jnp.sqrt(dist_sq)
    strength = mass_other * inverse * inverse * inverse
    radial = (offset_pos[0] * rel_vel[0] + offset_pos[1] * rel_vel[1] + offset_pos[2] * rel_vel[2]) / dist_sq
    accel = strength * offset_pos
    jerk_term = strength * (rel_vel - 3.0 * radial * offset_pos)
    return jnp.concatenate([accel, jerk_term], axis=0)

def predict(star_rows):
    position = star_rows[0:3] + time_step * (star_rows[3:6] + time_step * (0.5 * star_rows[6:9] + time_step * star_rows[9:12] / 6.0))
    velocity = star_rows[3:6] + time_step * (star_rows[6:9] + 0.5 * time_step * star_rows[9:12])
    return jnp.concatenate([position, velocity, star_rows[12:13]], axis=0)

def correct(own_state, total_sum):
    half_step = 0.5 * time_step
    twelfth = time_step * time_step / 12.0
    new_vel = own_state[3:6] + half_step * (own_state[6:9] + total_sum[0:3]) + twelfth * (own_state[9:12] - total_sum[3:6])
    new_pos = own_state[0:3] + half_step * (own_state[3:6] + new_vel) + twelfth * (own_state[6:9] - total_sum[0:3])
    return jnp.concatenate([new_pos, new_vel], axis=0)

def reference(star_state, active_local, neighbours, counts):
    predicted = predict(star_state)
    device_idx = jnp.arange(ACTIVES, dtype=jnp.int32) // A_DEV
    global_id = (device_idx // N_GRP * FIELD_DEV + active_local).astype(jnp.int32)
    own_state = jnp.take(star_state, global_id, axis=1)
    actives = jnp.take(predicted, global_id, axis=1)[0:6]
    act_blocks = actives.reshape(6, ACTIVES // A_DEV, A_DEV).transpose(1, 0, 2)

    def regular_block(act_block):
        pair_vals = pair_terms(act_block[0:3, :, None], act_block[3:6, :, None], predicted[0:3, None, :], predicted[3:6, None, :], predicted[6][None, :])
        return lax.optimization_barrier(jnp.sum(pair_vals, axis=-1))
    total_sum = lax.map(regular_block, act_blocks).transpose(1, 0, 2).reshape(6, ACTIVES)
    entries = jnp.take(predicted, neighbours, axis=1)
    pair_vals = pair_terms(actives[0:3, :, None], actives[3:6, :, None], entries[0:3], entries[3:6], entries[6])
    live_mask = jnp.arange(NB, dtype=jnp.int32)[None, :] < counts[:, None]
    irregular = lax.optimization_barrier(jnp.sum(jnp.where(live_mask[None], pair_vals, 0.0), axis=-1))
    return (correct(own_state, total_sum), total_sum - irregular, irregular)
```

```python
import jax
import jax.numpy as jnp
from jax import lax
from jax.experimental import pallas as pl
from jax.experimental.pallas import tpu as pltpu
from jax.sharding import Mesh, PartitionSpec as P

time_step = 0.0078125
soften_sq = 0.001

LANES = 128
ROWS = 4
CHUNK = 7 * ROWS
ACT = 64
HALF = ACT // 2
FAR = ("xl", "y", "z")


def column(row):
    on_diag = lax.broadcasted_iota(jnp.int32, (ACT, ACT), 0) == lax.broadcasted_iota(
        jnp.int32, (ACT, ACT), 1
    )
    spread = jnp.where(on_diag, jnp.broadcast_to(row, (ACT, ACT)).astype(jnp.float32), 0.0)
    return jnp.sum(spread, axis=1, keepdims=True).astype(jnp.int32)


def prep_kernel(copies, state_ref, local_ref, chunk_ref, own_ref):
    state = [state_ref[i : i + 1, :] for i in range(13)]
    predicted = []
    for i in range(3):
        predicted.append(
            state[i]
            + time_step
            * (
                state[3 + i]
                + time_step * (0.5 * state[6 + i] + time_step * state[9 + i] / 6.0)
            )
        )
    for i in range(3):
        predicted.append(state[3 + i] + time_step * (state[6 + i] + 0.5 * time_step * state[9 + i]))
    predicted.append(state[12])
    pieces = []
    for value in predicted:
        for q in range(ROWS):
            pieces.append(value[:, q * LANES : (q + 1) * LANES])
    chunk = jnp.concatenate(pieces, axis=0)
    for s in range(copies):
        chunk_ref[s] = chunk
    local = column(local_ref[...])
    lane = lax.broadcasted_iota(jnp.int32, (ACT, LANES), 1)
    picks = [jnp.broadcast_to(local, (ACT, LANES)) == lane + q * LANES for q in range(ROWS)]
    for i, value in enumerate(state[:12] + predicted[:6]):
        total = jnp.zeros((ACT, LANES), jnp.float32)
        for q in range(ROWS):
            row = jnp.broadcast_to(value[:, q * LANES : (q + 1) * LANES], (ACT, LANES))
            total = jnp.where(picks[q], row, total)
        own_ref[i] = jnp.broadcast_to(jnp.sum(total, axis=1, keepdims=True), (ACT, LANES))


def pair_terms(active, star):
    dx = [star[i] - active[i] for i in range(3)]
    dv = [star[3 + i] - active[3 + i] for i in range(3)]
    dist_sq = dx[0] * dx[0] + dx[1] * dx[1] + (dx[2] * dx[2] + soften_sq)
    inv = lax.rsqrt(dist_sq)
    inv_sq = inv * inv
    strength = (star[6] * inv) * inv_sq
    radial = (dx[0] * dv[0] + dx[1] * dv[1] + dx[2] * dv[2]) * inv_sq
    push = (3.0 * strength) * radial
    return [strength * d for d in dx] + [strength * dv[i] - push * dx[i] for i in range(3)]


def field_pass(parity, stars_ref, own_ref, near_ref, sums, rows):
    shards = stars_ref.shape[0]
    for part in range(4):
        active = [
            [own_ref[12 + i, (2 * part + g) * 8 : (2 * part + g + 1) * 8, :] for i in range(6)]
            for g in range(2)
        ]
        ids = near_ref[part * 8 : (part + 1) * 8, :]
        row_id = (ids >> 7) - parity * ROWS
        lane_id = ids & (LANES - 1)

        def step(s, carry):
            acc, found = carry
            acc = [list(a) for a in acc]
            found = list(found)
            for q in range(ROWS):
                star = [
                    jnp.broadcast_to(stars_ref[s, pl.ds(v * ROWS + q, 1), :], (8, LANES))
                    for v in range(7)
                ]
                hit = row_id == s * (2 * ROWS) + q
                for v in range(7):
                    value = jnp.take_along_axis(
                        star[v], lane_id, axis=1, mode="promise_in_bounds"
                    )
                    found[v] = jnp.where(hit, value, found[v])
                for g in range(2):
                    terms = pair_terms(active[g], star)
                    acc[g] = [a + t for a, t in zip(acc[g], terms)]
            return (tuple(tuple(a) for a in acc), tuple(found))

        init = (
            tuple(tuple(sums[i, 2 * part + g] for i in range(6)) for g in range(2)),
            tuple(rows[v, part] for v in range(7)),
        )
        yield part, lax.fori_loop(0, shards, step, init)


class Zero:
    def __getitem__(self, index):
        return jnp.zeros((8, LANES), jnp.float32)


class Tiles:
    def __init__(self, ref):
        self.ref = ref

    def __getitem__(self, index):
        first, tile = index
        return self.ref[first, tile * 8 : (tile + 1) * 8, :]


def first_kernel(core_ref, stars_ref, own_ref, near_ref, sum_ref, row_ref):
    parity = core_ref[0]
    for part, (acc, found) in field_pass(parity, stars_ref, own_ref, near_ref, Zero(), Zero()):
        for g in range(2):
            for i in range(6):
                sum_ref[i, (2 * part + g) * 8 : (2 * part + g + 1) * 8, :] = acc[g][i]
        for v in range(7):
            row_ref[v, part * 8 : (part + 1) * 8, :] = found[v]


def second_kernel(
    core_ref,
    stars_ref,
    own_ref,
    near_ref,
    sum_ref,
    row_ref,
    count_ref,
    new_ref,
    regular_ref,
    irregular_ref,
    total_sc,
    entry_sc,
):
    parity = 1 - core_ref[0]
    for part, (acc, found) in field_pass(
        parity, stars_ref, own_ref, near_ref, Tiles(sum_ref), Tiles(row_ref)
    ):
        for g in range(2):
            for i in range(6):
                total_sc[i, (2 * part + g) * 8 : (2 * part + g + 1) * 8, :] = acc[g][i]
        for v in range(7):
            entry_sc[v, part * 8 : (part + 1) * 8, :] = found[v]

    lane = lax.broadcasted_iota(jnp.int32, (HALF, LANES), 1)
    low = lane < HALF * 2
    count = column(count_ref[...])
    count = jnp.where(low, count[:HALF], count[HALF:])
    live = (lane & (ACT - 1)) < count
    active = [
        jnp.where(low, own_ref[12 + i, 0:HALF, :], own_ref[12 + i, HALF:ACT, :]) for i in range(6)
    ]
    terms = pair_terms(active, [entry_sc[v] for v in range(7)])
    irregular = []
    for term in terms:
        both = [
            jnp.sum(jnp.where(live & side, term, 0.0), axis=1, keepdims=True)
            for side in (low, jnp.logical_not(low))
        ]
        irregular.append(jnp.concatenate(both, axis=0))
    total = [jnp.sum(total_sc[i], axis=1, keepdims=True) for i in range(6)]
    own = [own_ref[i][:, 0:1] for i in range(12)]
    half_step = 0.5 * time_step
    twelfth = time_step * time_step / 12.0
    new_vel = [
        own[3 + i] + half_step * (own[6 + i] + total[i]) + twelfth * (own[9 + i] - total[3 + i])
        for i in range(3)
    ]
    new_pos = [
        own[i] + half_step * (own[3 + i] + new_vel[i]) + twelfth * (own[6 + i] - total[i])
        for i in range(3)
    ]
    regular = [total[i] - irregular[i] for i in range(6)]
    table = jnp.zeros((LANES, LANES), jnp.float32)
    column_id = lax.broadcasted_iota(jnp.int32, (ACT, LANES), 1)
    table = jnp.zeros((ACT, LANES), jnp.float32)
    for at, values in ((0, new_pos + new_vel), (8, regular), (16, irregular)):
        for i, value in enumerate(values):
            table = jnp.where(column_id == at + i, value, table)
    turned = jnp.concatenate([table, table], axis=0).T
    new_ref[...] = turned[0:6, 0:ACT]
    regular_ref[...] = turned[8:14, 0:ACT]
    irregular_ref[...] = turned[16:22, 0:ACT]


VM = pl.BlockSpec(memory_space=pltpu.VMEM)
SM = pl.BlockSpec(memory_space=pltpu.SMEM)


def shape(*dims):
    return jax.ShapeDtypeStruct(dims, jnp.float32)


def per_device(star_state, active_local, neighbours, counts):
    copies = lax.axis_size(FAR)
    chunks, own = pl.pallas_call(
        lambda *refs: prep_kernel(copies, *refs),
        out_shape=(shape(copies, CHUNK, LANES), shape(18, ACT, LANES)),
        in_specs=[VM, VM],
        out_specs=(VM, VM),
        name="prep",
    )(star_state, active_local.reshape(1, ACT))
    near = jnp.concatenate([neighbours[:HALF], neighbours[HALF:]], axis=1)
    core = lax.axis_index("c").astype(jnp.int32).reshape(1)
    mine = lax.all_to_all(chunks, FAR, 0, 0, tiled=True)
    other = lax.ppermute(mine, "c", [(0, 1), (1, 0)])
    stars = copies * ROWS * LANES
    cost = pl.CostEstimate(flops=45 * ACT * stars, bytes_accessed=28 * stars, transcendentals=0)
    sums, rows = pl.pallas_call(
        first_kernel,
        out_shape=(shape(6, ACT, LANES), shape(7, HALF, LANES)),
        in_specs=[SM, VM, VM, VM],
        out_specs=(VM, VM),
        cost_estimate=cost,
        name="first_half",
    )(core, mine, own, near)
    return pl.pallas_call(
        second_kernel,
        out_shape=(shape(6, ACT), shape(6, ACT), shape(6, ACT)),
        in_specs=[SM] + [VM] * 6,
        out_specs=(VM, VM, VM),
        scratch_shapes=[
            pltpu.VMEM((6, ACT, LANES), jnp.float32),
            pltpu.VMEM((7, HALF, LANES), jnp.float32),
        ],
        cost_estimate=cost,
        name="second_half",
    )(core, other, own, near, sums, rows, counts.reshape(1, ACT))


def solution(mesh):
    fine = Mesh(mesh.devices.reshape(2, 4, 4, 2, 2), ("xl", "y", "z", "c", "g"))
    blk = ("xl", "y", "z", "c")
    every = blk + ("g",)
    in_specs = (P(None, blk), P(every), P(every, None), P(every))
    out_specs = (P(None, every),) * 3
    return jax.shard_map(
        per_device, mesh=fine, in_specs=in_specs, out_specs=out_specs, check_vma=False
    )
```
